128 devices in a mesh: fsdp: 32 (over z_lo, x, y), dp: 4 (over z_hi, core).
Axes of the slice: x: 4, y: 4, z: 4 (z_hi: 2, z_lo: 2; z = z_hi * 2 + z_lo), core: 2. Of those that a mesh axis runs over, the one named last changes fastest.
Arguments:
- teacher_hidden: bfloat16 [1024, 8192], P(('fsdp', 'dp'))
- student_hidden: bfloat16 [1024, 4096], P(('fsdp', 'dp'))
- teacher_head: bfloat16 [8192, 65536], P('dp', 'fsdp'), may hold values from -0.1875 to 0.1875
- student_head: bfloat16 [4096, 65536], P('dp', 'fsdp'), may hold values from -0.25 to 0.25
- actions: int32 [1024], replicated, may hold values from 0 to 65535
- advantages: float32 [1024], replicated, may hold values from -0.21875 to 0.21875
- loss_mask: int32 [1024], replicated, may hold values 0 or 1
Outputs:
- token_loss: float32 [1024], P('dp')
- head_grad: float32 [4096, 65536], P('dp', 'fsdp')
- hidden_grad: bfloat16 [1024, 4096], P('fsdp', 'dp')
The draws below stay inside these ranges and needn't reach their ends.
All inputs are finite; a program needn't handle non-finite values.
Results may differ from the reference program's by a relative error of at most 0.0048.
Values may be sent and summed in bfloat16 or wider, within the bound.
No kernel may reach another device: no remote copies, remote signals or barrier semaphores. Data moves between devices by JAX's collectives and lax.ppermute only.
A program may use at most 128 MiB of HBM per device.

```python
import jax
import jax.numpy as jnp

DT = 8192
DS = 4096
VOCAB = 65536
TOKENS = 1024


def spread_rows(key, rows, cols):
    first, second = jax.random.split(key)
    values = jax.random.normal(first, (rows, cols), jnp.float32)
    scales = jnp.exp(jax.random.uniform(second, (rows,), jnp.float32, -1.3, -0.4))
    return values * scales[:, None]


def draw_teacher_hidden(key, part):
    return spread_rows(jax.random.fold_in(key, 11), TOKENS, DT).astype(jnp.bfloat16)


def draw_student_hidden(key, part):
    return spread_rows(jax.random.fold_in(key, 23), TOKENS, DS).astype(jnp.bfloat16)


def set_ends(array, stream_key, least, largest):
    place = [jax.random.randint(jax.random.fold_in(stream_key, axis), (), 0, length) for axis, length in enumerate(array.shape)]
    main_axis = array.shape.index(max(array.shape))
    neighbour = place[:main_axis] + [(place[main_axis] + 1) % array.shape[main_axis]] + place[main_axis + 1:]
    return array.at[tuple(place)].set(least).at[tuple(neighbour)].set(largest)


def block_levels(own_key, extent, shards, smallest, largest):
    def one(dim, shards_of):
        steps = jax.random.uniform(jax.random.fold_in(jax.random.fold_in(own_key, 6), dim), (shards_of,), jnp.float32, smallest / len(shards), largest / len(shards))
        return jnp.repeat(jnp.exp(steps), extent[dim] // shards_of).reshape((-1,) + (1,) * (len(extent) - dim - 1))

    loudness = one(*shards[0])
    for cut in shards[1:]:
        loudness = loudness * one(*cut)
    return loudness


def scatter_about(own_key, dims, scale, reach, shards=(), kind=jnp.bfloat16):
    gain = block_levels(own_key, dims, shards, -0.22, 0.18) if shards else 1.0
    array = jax.random.normal(own_key, dims, jnp.float32) * scale * gain
    return jnp.minimum(jnp.maximum(array, -reach), reach).astype(kind)


def setup_inputs(seed: int = 0) -> dict:
    arg_keys = jax.random.split(jax.random.key(seed), 8)
    teacher_hidden = draw_teacher_hidden(jax.random.fold_in(arg_keys[7], 71), 0)
    student_hidden = draw_student_hidden(jax.random.fold_in(arg_keys[7], 71), 0)
    teacher_head = scatter_about(arg_keys[2], (DT, VOCAB), (DT // 9) ** -0.5, 0.1875, ((0, 4), (1, 32)))
    student_head = scatter_about(arg_keys[3], (DS, VOCAB), (DS // 9) ** -0.5, 0.25, ((0, 4), (1, 32)))
    actions = set_ends(jax.random.randint(arg_keys[4], (TOKENS,), 0, VOCAB), jax.random.fold_in(arg_keys[4], 1), 0, VOCAB - 1).astype(jnp.int32)
    advantages = scatter_about(arg_keys[5], (TOKENS,), 0.015, 0.21875, (), jnp.float32)
    loss_mask = set_ends((jax.random.randint(arg_keys[6], (TOKENS,), 0, 4) < 3).astype(jnp.int32), jax.random.fold_in(arg_keys[6], 1), 0, 1)
    return dict(teacher_hidden=teacher_hidden, student_hidden=student_hidden, teacher_head=teacher_head, student_head=student_head, actions=actions, advantages=advantages, loss_mask=loss_mask)


kl_weight = 0.5


def reference(teacher_hidden, student_hidden, teacher_head, student_head, actions, advantages, loss_mask):
    teacher_logits = jnp.dot(teacher_hidden, teacher_head, preferred_element_type=jnp.float32)
    student_logits = jnp.dot(student_hidden, student_head, preferred_element_type=jnp.float32)
    teacher_max = jnp.max(teacher_logits, axis=1)
    student_max = jnp.max(student_logits, axis=1)
    teacher_exp = jnp.exp(teacher_logits - teacher_max[:, None])
    student_exp = jnp.exp(student_logits - student_max[:, None])
    teacher_sum = jnp.sum(teacher_exp, axis=1)
    student_sum = jnp.sum(student_exp, axis=1)
    teacher_lse = teacher_max + jnp.log(teacher_sum)
    student_lse = student_max + jnp.log(student_sum)
    teacher_prob = teacher_exp / teacher_sum[:, None]
    student_prob = student_exp / student_sum[:, None]
    kl = jnp.sum(teacher_prob * (teacher_logits - student_logits), axis=1) - teacher_lse + student_lse
    columns = jnp.arange(student_logits.shape[1], dtype=jnp.int32)
    onehot = (actions[:, None] == columns[None, :]).astype(jnp.float32)
    action_logp = jnp.sum(onehot * student_logits, axis=1) - student_lse
    weight = loss_mask.astype(jnp.float32)
    token_loss = weight * (kl_weight * kl - advantages * action_logp)
    logit_grad = (weight[:, None] * (kl_weight * (student_prob - teacher_prob) + advantages[:, None] * (student_prob - onehot))).astype(jnp.bfloat16)
    head_grad = jnp.dot(student_hidden.T, logit_grad, preferred_element_type=jnp.float32)
    hidden_grad = jnp.dot(logit_grad, student_head.T, preferred_element_type=jnp.float32).astype(jnp.bfloat16)
    return (token_loss, head_grad, hidden_grad)
```

```python
import jax
import jax.numpy as jnp
from jax import lax
from jax.sharding import PartitionSpec as P

kl_weight = 0.5
levels = 32767.0


def swap(x, bit):
    n = lax.axis_size("dp")
    return lax.ppermute(x, "dp", [(i, i ^ bit) for i in range(n)])


def spread(hidden):
    rows, width = hidden.shape
    quarters = lax.axis_size("dp")
    peers = lax.axis_size("fsdp")
    cut = hidden.reshape(rows, quarters, width // quarters).transpose(1, 0, 2)
    copies = jnp.broadcast_to(cut[:, None], (quarters, peers, rows, width // quarters))
    out = lax.all_to_all(
        copies.reshape(quarters * peers * rows, width // quarters),
        ("dp", "fsdp"),
        split_axis=0,
        concat_axis=0,
        tiled=True,
    )
    return out.reshape(quarters, peers * rows, width // quarters)


def block(x, index):
    return lax.dynamic_index_in_dim(x, index, 0, keepdims=False)


def product(x, head):
    return jnp.dot(x, head, preferred_element_type=jnp.float32)


def code(values):
    top = jnp.max(jnp.abs(values), axis=1, keepdims=True)
    ok = top > 1e-30
    step = jnp.where(ok, top / levels, 0.0)
    inverse = jnp.where(ok, levels / jnp.where(ok, top, 1.0), 0.0)
    return jnp.round(values * inverse).astype(jnp.int16), step


def partial_exchange(x, head, me):
    far_other = product(block(x, me ^ 3), head)
    far_got = swap(far_other, 1)
    far = product(block(x, me ^ 2), head) + far_got
    coded, step = code(far)
    coded_got, step_got = swap(coded, 2), swap(step, 2)
    near_other = product(block(x, me ^ 1), head)
    near_got = swap(near_other, 1)
    near = product(block(x, me), head) + near_got
    return near, coded_got, step_got, coded


def shards(
    teacher_hidden, student_hidden, teacher_head, student_head, actions, advantages, loss_mask
):
    me = lax.axis_index("dp")
    peers = lax.axis_size("fsdp")
    own_rows = teacher_hidden.shape[0]
    student_x = spread(student_hidden)
    student_near, student_coded, student_step, sent = partial_exchange(student_x, student_head, me)
    teacher_hidden, sent = lax.optimization_barrier((teacher_hidden, sent))
    teacher_x = spread(teacher_hidden)
    teacher_near, teacher_coded, teacher_step, _ = partial_exchange(teacher_x, teacher_head, me)
    student_logits = student_near + student_coded.astype(jnp.float32) * student_step
    teacher_logits = teacher_near + teacher_coded.astype(jnp.float32) * teacher_step

    def mine(a):
        return block(a.reshape(peers, -1, own_rows).transpose(1, 0, 2), me).reshape(-1)

    chosen, benefit = mine(actions), mine(advantages)
    weight = mine(loss_mask).astype(jnp.float32)
    vocab_shard = teacher_logits.shape[1]
    columns = lax.axis_index("fsdp") * vocab_shard + jnp.arange(vocab_shard, dtype=jnp.int32)
    onehot = (chosen[:, None] == columns[None, :]).astype(jnp.float32)
    teacher_top, student_top = jnp.max(teacher_logits, axis=1), jnp.max(student_logits, axis=1)
    teacher_exp = jnp.exp(teacher_logits - teacher_top[:, None])
    student_exp = jnp.exp(student_logits - student_top[:, None])
    stats = jnp.stack(
        [
            teacher_top,
            student_top,
            jnp.sum(teacher_exp, axis=1),
            jnp.sum(student_exp, axis=1),
            jnp.sum(teacher_exp * (teacher_logits - student_logits), axis=1),
            jnp.sum(onehot * student_logits, axis=1),
        ]
    )
    every = lax.all_to_all(
        jnp.broadcast_to(stats[None], (peers,) + stats.shape), "fsdp", 0, 0, tiled=True
    )
    teacher_max, student_max = jnp.max(every[:, 0], axis=0), jnp.max(every[:, 1], axis=0)
    teacher_part = jnp.exp(every[:, 0] - teacher_max)
    student_part = jnp.exp(every[:, 1] - student_max)
    teacher_sum = jnp.sum(every[:, 2] * teacher_part, axis=0)
    student_sum = jnp.sum(every[:, 3] * student_part, axis=0)
    cross = jnp.sum(every[:, 4] * teacher_part, axis=0)
    pick = jnp.sum(every[:, 5], axis=0)
    teacher_lse = teacher_max + jnp.log(teacher_sum)
    student_lse = student_max + jnp.log(student_sum)
    kl = cross / teacher_sum - teacher_lse + student_lse
    action_logp = pick - student_lse
    losses = weight * (kl_weight * kl - benefit * action_logp)
    teacher_prob = jnp.exp(teacher_logits - teacher_max[:, None]) * (1.0 / teacher_sum)[:, None]
    student_prob = jnp.exp(student_logits - student_max[:, None]) * (1.0 / student_sum)[:, None]
    grad = (
        weight[:, None]
        * (kl_weight * (student_prob - teacher_prob) + benefit[:, None] * (student_prob - onehot))
    ).astype(jnp.bfloat16)
    across = swap(grad, 2)
    beside = swap(grad, 1)
    grads = jnp.concatenate([grad, beside, across, swap(across, 1)], axis=0)
    student_rel = jnp.concatenate([block(student_x, me ^ i) for i in range(4)], axis=0)
    head_grad = lax.dot_general(
        student_rel, grads, (((0,), (0,)), ((), ())), preferred_element_type=jnp.float32
    )
    hidden_part = lax.dot_general(
        grads, student_head, (((1,), (1,)), ((), ())), preferred_element_type=jnp.float32
    ).astype(jnp.bfloat16)
    features = hidden_part.shape[1]
    hidden_part = hidden_part.reshape(4, peers, own_rows, features).transpose(1, 0, 2, 3)
    parts = lax.all_to_all(
        hidden_part.reshape(peers * 4 * own_rows, features), "fsdp", 0, 0, tiled=True
    )
    summed = jnp.sum(parts.reshape(peers, 4, own_rows, features).astype(jnp.float32), axis=0)

    def absolute(rel):
        return jnp.stack([block(rel, me ^ i) for i in range(4)])

    hidden_grad = absolute(summed).reshape(4 * own_rows, features).astype(jnp.bfloat16)
    pair = jnp.stack([losses, swap(losses, 1)])
    all_losses = absolute(jnp.concatenate([pair, swap(pair, 2)], axis=0))
    out_peers = peers // 4
    all_losses = lax.dynamic_slice_in_dim(
        all_losses.reshape(4, peers, own_rows), me * out_peers, out_peers, axis=1
    )
    token_loss = all_losses.transpose(1, 0, 2).reshape(-1)
    return (token_loss, head_grad, hidden_grad)


def solution(mesh):
    placed = (
        P(("fsdp", "dp"), None),
        P(("fsdp", "dp"), None),
        P("dp", "fsdp"),
        P("dp", "fsdp"),
        P(),
        P(),
        P(),
    )
    return jax.shard_map(
        shards,
        mesh=mesh,
        in_specs=placed,
        out_specs=(P("dp"), P("dp", "fsdp"), P("fsdp", "dp")),
        check_vma=False,
    )
```
